32 devices in a mesh: ctx: 8 (over z, y), fsdp: 4 (over x, core).
Axes of the slice: x: 2, y: 2, z: 4, core: 2. Of those that a mesh axis runs over, the one named last changes fastest.
Arguments:
- inputs: bfloat16 [4, 1536, 256], P('fsdp', 'ctx'), may hold values from -6 to 6
- positions: int32 [4, 1536], P('fsdp', 'ctx'), may hold values from 0 to 1535, as said below
- cotangent: bfloat16 [4, 1536, 256], P('fsdp', 'ctx'), may hold values from -6 to 6
- parameters: float32 [789760], P(('ctx', 'fsdp')), may hold values from -1.8 to 1.9
- first_moment: float32 [789760], P(('ctx', 'fsdp')), may hold values from -8 to 8
- second_moment: float32 [789760], P(('ctx', 'fsdp')), may hold values from 0.05 to 50
Outputs:
- outputs: bfloat16 [4, 1536, 256], P('fsdp', 'ctx')
- input_grad: float32 [4, 1536, 256], P('fsdp', 'ctx')
- param_grad: float32 [789760], P(('ctx', 'fsdp'))
- new_parameters: float32 [789760], P(('ctx', 'fsdp'))
- new_first: float32 [789760], P(('ctx', 'fsdp'))
- new_second: float32 [789760], P(('ctx', 'fsdp'))
The draws below stay inside these ranges and needn't reach their ends.
Inputs may be any that keep to these rules, and one draw needn't show every extreme that they name: In each sequence the positions are a permutation of 0 to 1535 in which every aligned run of 192 entries holds 192 consecutive positions in increasing order.
All inputs are finite; a program needn't handle non-finite values.
Results may differ from the reference program's by a relative error of at most 0.012.
The reference program's roundings to bfloat16 on the way count: a program that leaves them out, or rounds other values in their place, can miss the bound.
Values may be sent and summed in bfloat16 or wider, within the bound.
No kernel may reach another device: no remote copies, remote signals or barrier semaphores. Data moves between devices by JAX's collectives and lax.ppermute only.
A program may use at most 64 MiB of HBM per device.

```python
import math
import jax
import jax.numpy as jnp
from jax import lax

D = 256
FF = 1024
HEADS = 8
HEAD = 32
ROT = 8
STEP = 10
TOK_DEV = 192
SEQS = 4
LENGTH = 1536
PARAMS = 789760


def draw_positions(key, part):
    blocks = LENGTH // TOK_DEV
    keys = jax.random.split(key, SEQS)
    order = jax.vmap(lambda single: jax.random.permutation(single, blocks))(keys)
    within = jnp.arange(TOK_DEV, dtype=jnp.int32)
    return (order.astype(jnp.int32)[:, :, None] * TOK_DEV + within[None, None, :]).reshape(SEQS, LENGTH)


def draw_parameters(key, part):
    noise = jnp.clip(jax.random.normal(key, (PARAMS,), jnp.float32), -6.0, 6.0)
    root_d = float(D) ** 0.5
    root_f = float(FF) ** 0.5
    column_scale = jnp.concatenate([jnp.full((2 * D,), 1.6, jnp.float32), jnp.full((D,), 1.0, jnp.float32)]) / root_d
    scales = jnp.concatenate([jnp.full((D,), 0.15, jnp.float32), jnp.full((D,), 0.3, jnp.float32), jnp.full((D,), 0.15, jnp.float32), jnp.full((D,), 0.3, jnp.float32), jnp.full((3 * D,), 0.3, jnp.float32), jnp.full((D,), 0.3, jnp.float32), jnp.full((FF,), 0.3, jnp.float32), jnp.full((D,), 0.3, jnp.float32), jnp.tile(column_scale, D), jnp.full((D * D,), 2.0 / root_d, jnp.float32), jnp.full((D * FF,), 1.0 / root_d, jnp.float32), jnp.full((FF * D,), 1.5 / root_f, jnp.float32)])
    base = jnp.concatenate([jnp.ones((D,), jnp.float32), jnp.zeros((D,), jnp.float32), jnp.ones((D,), jnp.float32), jnp.zeros((PARAMS - 3 * D,), jnp.float32)])
    return noise * scales + base


def steps_of(rng, shape, cuts, smallest, top_value):
    loudness = 1.0
    for dim, shards_of in cuts:
        heights = jax.random.uniform(jax.random.fold_in(jax.random.fold_in(rng, 6), dim), (shards_of,), jnp.float32, smallest / len(cuts), top_value / len(cuts))
        loudness = loudness * jnp.repeat(jnp.exp(heights), shape[dim] // shards_of).reshape((-1,) + (1,) * (len(shape) - 1 - dim))
    return loudness


def bell_draw(own_key, shape, scale, limit, cuts=(), kind=jnp.bfloat16):
    drawn = scale * jax.random.normal(own_key, shape, jnp.float32)
    if cuts:
        drawn = drawn * steps_of(own_key, shape, cuts, -0.22, 0.18)
    return jnp.clip(drawn, -limit, limit).astype(kind)


def setup_inputs(seed: int = 0) -> dict:
    streams_of = jax.random.split(jax.random.key(seed), 7)
    inputs = bell_draw(streams_of[0], (SEQS, LENGTH, D), 1.0, 6.0, ((0, 4), (1, 8)))
    positions = draw_positions(jax.random.fold_in(streams_of[6], 71), 0)
    cotangent = bell_draw(streams_of[2], (SEQS, LENGTH, D), 1.0, 6.0, ((0, 4), (1, 8)))
    parameters = draw_parameters(jax.random.fold_in(streams_of[6], 71), 0)
    first_moment = bell_draw(streams_of[4], (PARAMS,), 2.0, 8.0, ((0, 32),), jnp.float32)
    second_moment = jnp.clip(jnp.exp(math.log(50.0) - 6.9077553 * jax.random.uniform(streams_of[5], (PARAMS,), jnp.float32) ** steps_of(streams_of[5], (PARAMS,), ((0, 32),), -0.2, 0.2)), 0.05, 50.0)
    return dict(inputs=inputs, positions=positions, cotangent=cotangent, parameters=parameters, first_moment=first_moment, second_moment=second_moment)


@jax.custom_vjp
def low(v):
    return lax.optimization_barrier(v.astype(jnp.bfloat16)).astype(jnp.float32)

@jax.custom_vjp
def low_back(v):
    return v

def low_keep(v):
    return (low(v), None)

def low_pass(kept, grad):
    return (grad,)

def back_keep(v):
    return (v, None)

def back_low(kept, grad):
    return (low(grad),)
low.defvjp(low_keep, low_pass)
low_back.defvjp(back_keep, back_low)
first_beta = 0.9
second_beta = 0.999
learn_rate = 0.02
weight_decay = 0.1
epsilon = 1e-08

def layout():
    return [(D,), (D,), (D,), (D,), (3 * D,), (D,), (FF,), (D,), (D, 3 * D), (D, D), (D, FF), (FF, D)]

def unpack(flat):
    pieces = []
    offset = 0
    for shape in layout():
        extent = math.prod(shape)
        pieces.append(flat[offset:offset + extent].reshape(shape))
        offset += extent
    return pieces

def layer_norm(values, gain, shift):
    center = lax.optimization_barrier(jnp.mean(values, axis=-1, keepdims=True))
    centered = values - center
    spread = lax.optimization_barrier(jnp.mean(centered * centered, axis=-1, keepdims=True))
    return centered * lax.rsqrt(spread + 1e-05) * gain + shift

def angles(places):
    half = ROT // 2
    freqs = 10000.0 ** (-2.0 * jnp.arange(half, dtype=jnp.float32) / ROT)
    theta = places.astype(jnp.float32)[:, None] * freqs[None, :]
    return (jnp.cos(theta), jnp.sin(theta))

def rotate(heads, cosine, sine):
    half = ROT // 2
    first = heads[..., :half]
    second = heads[..., half:ROT]
    cosine = cosine[:, None, :]
    sine = sine[:, None, :]
    return jnp.concatenate([first * cosine - second * sine, second * cosine + first * sine, heads[..., ROT:]], axis=-1)

def attend(query, key, value, places):
    length = query.shape[0]
    block = 512 if length % 512 == 0 else length
    number = length // block
    scale = HEAD ** (-0.5)

    def one_block(item):
        query_block, place_block = item
        scores = jnp.einsum('qhd,khd->hqk', query_block, key, precision=lax.Precision.HIGHEST) * scale
        scores = low_back(scores)
        allowed = places[None, :] <= place_block[:, None]
        scores = jnp.where(allowed[None], scores, -1e+30)
        probs = low(jax.nn.softmax(scores, axis=-1))
        return jnp.einsum('hqk,khd->qhd', probs, value, precision=lax.Precision.HIGHEST)
    mixed = lax.map(jax.checkpoint(one_block), (query.reshape(number, block, HEADS, HEAD), places.reshape(number, block)))
    return mixed.reshape(length, HEADS, HEAD)

def forward(tokens, places, flat):
    gain_one, shift_one, gain_two, shift_two, qkv_bias, out_bias, up_bias, down_bias, qkv_weight, out_weight, up_weight, down_weight = unpack(low(flat))
    length = tokens.shape[0]
    normed_one = low(layer_norm(tokens, gain_one, shift_one))
    normed_two = low(layer_norm(tokens, gain_two, shift_two))
    projected = low_back(jnp.dot(normed_one, qkv_weight, precision=lax.Precision.HIGHEST) + qkv_bias)
    cosine, sine = angles(places)
    query = low(rotate(projected[:, :D].reshape(length, HEADS, HEAD), cosine, sine))
    key = low(rotate(projected[:, D:2 * D].reshape(length, HEADS, HEAD), cosine, sine))
    value = low(projected[:, 2 * D:].reshape(length, HEADS, HEAD))
    attended = attend(query, key, value, places).reshape(length, D)
    attended = low(low_back(attended))
    hidden_pre = low_back(jnp.dot(normed_two, up_weight, precision=lax.Precision.HIGHEST) + up_bias)
    hidden = low(jax.nn.gelu(hidden_pre, approximate=False))
    attn_branch = jnp.dot(attended, out_weight, precision=lax.Precision.HIGHEST) + out_bias
    mlp_branch = jnp.dot(hidden, down_weight, precision=lax.Precision.HIGHEST) + down_bias
    return tokens + attn_branch + mlp_branch

def reference(inputs, positions, cotangent, parameters, first_moment, second_moment):

    def one_sequence(running, item):
        values, places, grad_out = item
        result, pull = jax.vjp(lambda tokens, flat: forward(tokens, places, flat), values.astype(jnp.float32), parameters)
        token_grad, flat_grad = pull(grad_out.astype(jnp.float32))
        return (running + flat_grad, (result.astype(jnp.bfloat16), token_grad))
    param_grad, (outputs, input_grad) = lax.scan(one_sequence, jnp.zeros((PARAMS,), jnp.float32), (inputs, positions, cotangent))
    new_first = first_beta * first_moment + (1.0 - first_beta) * param_grad
    new_second = second_beta * second_moment + (1.0 - second_beta) * param_grad * param_grad
    first_hat = new_first / (1.0 - first_beta ** STEP)
    second_hat = new_second / (1.0 - second_beta ** STEP)
    new_parameters = parameters - learn_rate * (first_hat / (jnp.sqrt(second_hat) + epsilon) + weight_decay * parameters)
    return (outputs, input_grad, param_grad, new_parameters, new_first, new_second)
```

```python
import functools
import math

import jax
import jax.numpy as jnp
import numpy as np
from jax import lax
from jax.experimental import pallas as pl
from jax.experimental.pallas import tpu as pltpu
from jax.sharding import PartitionSpec as P

D = 256
FF = 1024
HEADS = 8
HEAD = 32
ROT = 8
STEP = 10
LANES = 128

first_beta = 0.9
second_beta = 0.999
learn_rate = 0.02
weight_decay = 0.1
epsilon = 1e-08

ROW_GAIN_ONE, ROW_SHIFT_ONE, ROW_GAIN_TWO, ROW_SHIFT_TWO = 0, 2, 4, 6
ROW_QKV_BIAS, ROW_OUT_BIAS, ROW_UP_BIAS, ROW_DOWN_BIAS = 8, 14, 16, 24
ROW_QKV, ROW_OUT, ROW_UP, ROW_DOWN = 26, 1562, 2074, 4122
ROW_END = 6170


f32 = jnp.float32
bf16 = jnp.bfloat16


def nt(a, b):
    return lax.dot_general(a, b, (((1,), (1,)), ((), ())), preferred_element_type=f32)


def tn(a, b):
    return lax.dot_general(a, b, (((0,), (0,)), ((), ())), preferred_element_type=f32)


def nn(a, b):
    return lax.dot_general(a, b, (((1,), (0,)), ((), ())), preferred_element_type=f32)


def normalize(values):
    center = jnp.mean(values, axis=-1, keepdims=True)
    centered = values - center
    spread = jnp.mean(centered * centered, axis=-1, keepdims=True)
    inverse = lax.rsqrt(spread + 1e-05)
    return centered * inverse, inverse


def wide_row(ref, row):
    return jnp.concatenate([ref[row : row + 1, :], ref[row + 1 : row + 2, :]], axis=1)


def put_row(ref, row, value):
    for k in range(value.shape[1] // LANES):
        ref[row + k : row + k + 1, :] = value[:, k * LANES : (k + 1) * LANES]


def main_kernel(members, owners, slot_rows, rows, info, starts, slots, *refs):
    xs = refs[:members]
    cots = refs[members : 2 * members]
    (rope, sums, payload, base, second_part, turned, out_low, vectors) = refs[
        2 * members : 2 * members + 8
    ]
    (flat, grads, up_low, down_low, normed, hat, cot_all, q_t, k_t, v_t, g_t, dk_t, dv_t, result, tile) = refs[
        2 * members + 8 :
    ]
    length = members * rows
    head = info[0]
    active = info[1].astype(f32)

    flat[...] = jnp.zeros_like(flat)

    def place(a, carry):
        flat[pl.ds(starts[a], slot_rows), :] += slots[a].astype(f32)
        return carry

    lax.fori_loop(0, owners, place, 0, unroll=4)

    for g in range(6):
        piece = flat[pl.ds(ROW_QKV + g, D, stride=6), :]
        turned[g * LANES : (g + 1) * LANES, :D] = piece.T.astype(bf16)
        bias = jnp.broadcast_to(flat[ROW_QKV_BIAS + g : ROW_QKV_BIAS + g + 1, :], (LANES, LANES))
        turned[g * LANES : (g + 1) * LANES, D : D + LANES] = bias.T.astype(bf16)
    for k in range(2):
        cols = slice(k * LANES, (k + 1) * LANES)
        out_low[:, cols] = flat[pl.ds(ROW_OUT + k, D, stride=2), :].astype(bf16)
        down_low[:, cols] = flat[pl.ds(ROW_DOWN + k, FF, stride=2), :].astype(bf16)
    for k in range(FF // LANES):
        up_low[:, k * LANES : (k + 1) * LANES] = flat[
            pl.ds(ROW_UP + k, D, stride=FF // LANES), :
        ].astype(bf16)
    vectors[...] = flat[:32, :]

    grads[:ROW_UP, :] = jnp.zeros((ROW_UP, LANES), f32)
    grads[ROW_END:, :] = jnp.zeros((grads.shape[0] - ROW_END, LANES), f32)

    tokens = xs[0][:rows, :].astype(f32)
    hat_own, unused = normalize(tokens)
    gain_two = wide_row(flat, ROW_GAIN_TWO)
    second_low = (hat_own * gain_two + wide_row(flat, ROW_SHIFT_TWO)).astype(bf16)
    cot_own = cots[0][...]
    up_bias = jnp.concatenate([flat[ROW_UP_BIAS + k : ROW_UP_BIAS + k + 1, :] for k in range(FF // LANES)], axis=1)
    pre = nn(second_low, up_low[...]) + up_bias
    cdf = 0.5 * (1.0 + lax.erf(pre * (2.0**-0.5)))
    hidden = (pre * cdf).astype(bf16)
    slope = cdf + pre * (jnp.exp(pre * pre * -0.5) * ((2.0 * math.pi) ** -0.5))
    base[...] = (
        tokens
        + nn(hidden, down_low[...])
        + (wide_row(flat, ROW_OUT_BIAS) + wide_row(flat, ROW_DOWN_BIAS))
    )
    hidden_grad = (nt(cot_own, down_low[...]) * slope).astype(bf16)
    down_grad = tn(hidden, cot_own)
    for k in range(2):
        grads[pl.ds(ROW_DOWN + k, FF, stride=2), :] = down_grad[:, k * LANES : (k + 1) * LANES]
    up_grad = tn(second_low, hidden_grad)
    for k in range(FF // LANES):
        grads[pl.ds(ROW_UP + k, D, stride=FF // LANES), :] = up_grad[:, k * LANES : (k + 1) * LANES]
    put_row(grads, ROW_UP_BIAS, jnp.sum(hidden_grad.astype(f32), axis=0, keepdims=True))
    bias_grad = jnp.sum(cot_own.astype(f32), axis=0, keepdims=True)
    put_row(grads, ROW_OUT_BIAS, bias_grad)
    put_row(grads, ROW_DOWN_BIAS, bias_grad)
    second_grad = nt(hidden_grad, up_low[...])
    put_row(grads, ROW_GAIN_TWO, jnp.sum(second_grad * hat_own, axis=0, keepdims=True))
    put_row(grads, ROW_SHIFT_TWO, jnp.sum(second_grad, axis=0, keepdims=True))
    second_part[...] = second_grad * gain_two

    gain_one = wide_row(flat, ROW_GAIN_ONE)
    shift_one = wide_row(flat, ROW_SHIFT_ONE)
    places = []
    for k in range(members):
        rank = jnp.max(xs[k][rows : rows + 16, :LANES].astype(f32)).astype(jnp.int32)
        place_at = pl.multiple_of(rank * rows, 16)
        places.append(place_at)
        here, unused = normalize(xs[k][:rows, :].astype(f32))
        hat[pl.ds(place_at, rows), :] = here.astype(bf16)
        normed[pl.ds(place_at, rows), :] = (here * gain_one + shift_one).astype(bf16)
        cot_all[pl.ds(place_at, rows), :] = cots[k][...]

    at = pl.multiple_of(head * HEAD, HEAD)
    weight_head = [turned[pl.ds(s * D + at, HEAD), :] for s in range(3)]
    cosine = rope[:8, :]
    sine = rope[8:, :]
    for s, target in enumerate((q_t, k_t, v_t)):
        made = nt(weight_head[s][:, :D], normed[...]) + weight_head[s][:, D : D + 1].astype(f32)
        if s < 2:
            top = made[:8, :]
            top = top * cosine + pltpu.roll(top, 4, 0) * sine
            made = jnp.concatenate([top, made[8:, :]], axis=0)
        target[...] = made.astype(bf16)
    g_t[...] = nt(out_low[pl.ds(at, HEAD), :], cot_all[...]).astype(bf16)

    dk_t[...] = jnp.zeros_like(dk_t)
    dv_t[...] = jnp.zeros_like(dv_t)
    span = tile.shape[1]
    count = length // span
    scale = HEAD ** (-0.5)
    factor = scale * math.log2(math.e)
    causal = lax.broadcasted_iota(jnp.int32, (span, span), 0) <= lax.broadcasted_iota(
        jnp.int32, (span, span), 1
    )
    static = count <= 4

    def cut(i):
        if static:
            return pl.ds(i * span, span)
        return pl.ds(pl.multiple_of(i * span, span), span)

    def loop(stop, body, carry):
        if static:
            for j in range(stop):
                carry = body(j, carry)
            return carry
        return lax.fori_loop(0, stop, body, carry)

    def query_tile(i, unused):
        mine = cut(i)
        query = q_t[:, mine]
        grad = g_t[:, mine]

        def score(j, top, last=False):
            values = tn(k_t[:, cut(j)], query)
            if last:
                values = jnp.where(causal, values, -1e30)
            tile[cut(j), :] = values
            return jnp.maximum(top, jnp.max(values, axis=0, keepdims=True))

        top = loop(i, score, jnp.full((1, span), -1e30, f32))
        top = score(i, top, True) * factor

        def weigh(j, carry):
            total, mixed = carry
            weights = jnp.exp2(tile[cut(j), :] * factor - top)
            tile[cut(j), :] = weights
            return (
                total + jnp.sum(weights, axis=0, keepdims=True),
                mixed + nn(v_t[:, cut(j)], weights.astype(bf16)),
            )

        total, mixed = loop(
            i + 1, weigh, (jnp.zeros((1, span), f32), jnp.zeros((HEAD, span), f32))
        )
        part = 1.0 / total
        attended = mixed * part
        delta = jnp.sum(grad.astype(f32) * attended, axis=0, keepdims=True)

        def back(j, query_grad):
            prob = tile[cut(j), :] * part
            change = (prob * (tn(v_t[:, cut(j)], grad) - delta)).astype(bf16)
            dv_t[:, cut(j)] += nt(grad, prob.astype(bf16))
            dk_t[:, cut(j)] += nt(query, change)
            return query_grad + nn(k_t[:, cut(j)], change)

        query_grad = loop(i + 1, back, jnp.zeros((HEAD, span), f32))
        result[:HEAD, mine] = attended
        result[HEAD : 2 * HEAD, mine] = query_grad * scale
        return unused

    loop(count, query_tile, 0)

    def turn_back(made):
        top = made[:8, :]
        top = top * cosine - pltpu.roll(top, 4, 0) * sine
        return jnp.concatenate([top, made[8:, :]], axis=0)

    result[HEAD : 2 * HEAD, :] = turn_back(result[HEAD : 2 * HEAD, :])
    result[2 * HEAD : 3 * HEAD, :] = turn_back(dk_t[...] * scale)
    result[3 * HEAD :, :] = dv_t[...]
    low_t = result[...].astype(bf16)
    weight_grad_t = nn(low_t, normed[...])
    gain_sum_t = nn(low_t, hat[...])
    out_grad = nn(low_t, cot_all[...])[:HEAD, :] * active
    bias_row = nt(jnp.ones((8, length), bf16), low_t)[:1, :]
    bias_col = jnp.sum(low_t.astype(f32), axis=1, keepdims=True)
    weight_all = jnp.concatenate([w[:, :D].astype(f32) for w in weight_head], axis=0)
    put_row(
        grads,
        ROW_GAIN_ONE,
        jnp.sum(weight_all * gain_sum_t[HEAD:, :], axis=0, keepdims=True) * active,
    )
    put_row(
        grads,
        ROW_SHIFT_ONE,
        jnp.sum(weight_all * bias_col[HEAD:, :], axis=0, keepdims=True) * active,
    )
    weight_grad = weight_grad_t.T
    lane_at = (head % 4) * HEAD
    for s in range(3):
        shift = (lane_at + (96 - HEAD * s)) % LANES
        moved = pltpu.roll(weight_grad, shift, 1)
        moved_bias = pltpu.roll(jnp.broadcast_to(bias_row, (8, LANES)), shift, 1)
        for half in range(2):
            lane = lax.broadcasted_iota(jnp.int32, (1, LANES), 1)
            keep = ((lane >= lane_at) & (lane < lane_at + HEAD)).astype(f32)
            keep = keep * (active * (head // 4 == half).astype(f32))
            g = 2 * s + half
            grads[pl.ds(ROW_QKV + g, D, stride=6), :] = moved * keep
            grads[ROW_QKV_BIAS + g : ROW_QKV_BIAS + g + 1, :] = moved_bias[:1, :] * keep
    for k in range(2):
        grads[pl.ds(ROW_OUT + 2 * HEAD * head + k, HEAD, stride=2), :] = out_grad[
            :, k * LANES : (k + 1) * LANES
        ]

    def emit(a, carry):
        sums[a] = grads[pl.ds(starts[a], slot_rows), :].astype(bf16)
        return carry

    lax.fori_loop(0, owners, emit, 0, unroll=4)

    normed[:, :LANES] = result[...].T.astype(bf16)
    for k in range(members):
        payload[k] = normed[pl.ds(places[k], rows), :LANES]


def final_kernel(members, rows, heads, *refs):
    parts = refs[:members]
    (base, second_part, turned, out_low, vectors, own, cot) = refs[members : members + 7]
    outputs, input_grad = refs[members + 7 : members + 9]
    both = refs[members + 9]
    both[...] = jnp.zeros_like(both)
    for k in range(members):

        @pl.when(heads[k] < HEADS)
        def _():
            at = pl.multiple_of(heads[k] * HEAD, HEAD)
            empty = jnp.zeros((HEAD, D), bf16)
            left = jnp.concatenate([out_low[pl.ds(at, HEAD), :], empty, empty, empty], axis=0)
            right = jnp.concatenate(
                [empty] + [turned[pl.ds(s * D + at, HEAD), :D] for s in range(3)], axis=0
            )
            both[...] += nn(parts[k][...], jnp.concatenate([left, right], axis=1))

    outputs[...] = (base[...] + both[:, :D]).astype(bf16)
    e = both[:, D:] * wide_row(vectors, ROW_GAIN_ONE) + second_part[...]
    hat, inverse = normalize(own[:rows, :].astype(f32))
    middle = jnp.mean(e, axis=-1, keepdims=True)
    slant = jnp.mean(e * hat, axis=-1, keepdims=True)
    input_grad[...] = cot[...].astype(f32) + inverse * (e - middle - hat * slant)


def per_device(ctx, fsdp, inputs, positions, cotangent, parameters, first_moment, second_moment):
    members, owners = ctx, ctx * fsdp
    rows = inputs.shape[1]
    length = members * rows
    shard = parameters.shape[0]
    slot_rows = -(-(shard + LANES - 1) // LANES)
    slot_rows = -(-slot_rows // 16) * 16
    low_bits = fsdp.bit_length() - 1
    bits = owners.bit_length() - 1
    gather_order = list(range(low_bits + 1, bits)) + [low_bits] + list(range(low_bits - 1, -1, -1))
    gather_order = [b for b in gather_order if b < bits]

    member = lax.axis_index("ctx")
    me = member * fsdp + lax.axis_index("fsdp")

    def swapped(block, bit):
        if bit < low_bits:
            return lax.ppermute(block, "fsdp", [(i, i ^ (1 << bit)) for i in range(fsdp)])
        step = 1 << (bit - low_bits)
        return lax.ppermute(block, "ctx", [(i, i ^ step) for i in range(ctx)])

    slot_owner = np.zeros(owners, np.int32)
    for a in range(owners):
        for s, bit in enumerate(gather_order):
            slot_owner[a] |= ((a >> s) & 1) << bit
    table = (np.arange(owners)[:, None] ^ slot_owner[None, :]) * shard // LANES
    starts = jnp.asarray(table, jnp.int32)[me]
    offset = (me * shard) % LANES

    shifted = lax.dynamic_update_slice(
        jnp.zeros((slot_rows * LANES,), f32), parameters, (offset,)
    )
    slots = shifted.reshape(1, slot_rows, LANES).astype(bf16)
    for bit in gather_order:
        slots = jnp.concatenate([slots, swapped(slots, bit)], axis=0)

    ring = list(range(0, ctx, 2)) + list(range(1, ctx, 2))[::-1]
    pos_table = np.zeros(ctx, np.int32)
    for p, c in enumerate(ring):
        pos_table[c] = p
    ring_at = jnp.asarray(pos_table)[member]

    def along(block, distance):
        return lax.ppermute(
            block, "ctx", [(ring[p], ring[(p + distance) % ctx]) for p in range(ctx)]
        )

    rank = (positions[0, :1] // rows).astype(bf16)
    message = jnp.concatenate(
        [inputs[0], jnp.broadcast_to(rank[:, None], (16, D))], axis=0
    )
    xs = [None] * members
    cots = [None] * members
    xs[0], cots[0] = message, cotangent[0]
    ahead = (message, cotangent[0])
    behind = (message, cotangent[0])
    for step in range(1, members // 2 + 1):
        ahead = tuple(along(v, 1) for v in ahead)
        xs[members - step], cots[members - step] = ahead
        if step < members - step:
            behind = tuple(along(v, -1) for v in behind)
            xs[step], cots[step] = behind

    half = ROT // 2
    freqs = 10000.0 ** (-2.0 * jnp.arange(half, dtype=f32) / ROT)
    theta = freqs[:, None] * jnp.arange(length, dtype=f32)[None, :]
    cosine, sine = jnp.cos(theta), jnp.sin(theta)
    rope = jnp.concatenate([cosine, cosine, -sine, sine], axis=0)

    head = member % HEADS
    info = jnp.stack([head, (member < HEADS).astype(jnp.int32)])
    flat_rows = -(-(ROW_END + slot_rows) // 16) * 16
    span = 2 * rows
    vmem = pl.BlockSpec(memory_space=pltpu.VMEM)
    smem = pl.BlockSpec(memory_space=pltpu.SMEM)
    limit = pltpu.CompilerParams(vmem_limit_bytes=60 * 1024 * 1024)
    sums, payload, base, second_part, turned, out_low, vectors = pl.pallas_call(
        functools.partial(main_kernel, members, owners, slot_rows, rows),
        out_shape=(
            jax.ShapeDtypeStruct((owners, slot_rows, LANES), bf16),
            jax.ShapeDtypeStruct((members, rows, LANES), bf16),
            jax.ShapeDtypeStruct((rows, D), f32),
            jax.ShapeDtypeStruct((rows, D), f32),
            jax.ShapeDtypeStruct((3 * D, D + LANES), bf16),
            jax.ShapeDtypeStruct((D, D), bf16),
            jax.ShapeDtypeStruct((32, LANES), f32),
        ),
        in_specs=[smem, smem] + [vmem] * (2 + 2 * members),
        out_specs=(vmem,) * 7,
        scratch_shapes=[
            pltpu.VMEM((flat_rows, LANES), f32),
            pltpu.VMEM((flat_rows, LANES), f32),
            pltpu.VMEM((D, FF), bf16),
            pltpu.VMEM((FF, D), bf16),
            pltpu.VMEM((length, D), bf16),
            pltpu.VMEM((length, D), bf16),
            pltpu.VMEM((length, D), bf16),
            pltpu.VMEM((HEAD, length), bf16),
            pltpu.VMEM((HEAD, length), bf16),
            pltpu.VMEM((HEAD, length), bf16),
            pltpu.VMEM((HEAD, length), bf16),
            pltpu.VMEM((HEAD, length), f32),
            pltpu.VMEM((HEAD, length), f32),
            pltpu.VMEM((LANES, length), f32),
            pltpu.VMEM((length, span), f32),
        ],
        compiler_params=limit,
        name="layer",
    )(info, starts, slots, *xs, *cots, rope)

    held = sums
    for bit in gather_order[::-1]:
        middle = held.shape[0] // 2
        arrived = swapped(held[middle:].astype(bf16), bit)
        held = held[:middle].astype(f32) + arrived.astype(f32)
    parts = [payload[0]] + [along(payload[k], k) for k in range(1, members)]
    heads = jnp.asarray(
        np.array([[ring[(p - k) % ctx] for k in range(ctx)] for p in range(ctx)], np.int32)
    )[ring_at]
    outputs, input_grad = pl.pallas_call(
        functools.partial(final_kernel, members, rows),
        out_shape=(
            jax.ShapeDtypeStruct((rows, D), bf16),
            jax.ShapeDtypeStruct((rows, D), f32),
        ),
        in_specs=[smem] + [vmem] * (members + 7),
        out_specs=(vmem, vmem),
        scratch_shapes=[pltpu.VMEM((rows, 2 * D), f32)],
        compiler_params=limit,
        name="finish",
    )(heads, *parts, base, second_part, turned, out_low, vectors, message, cotangent[0])

    param_grad = lax.dynamic_slice(held.reshape(-1), (offset,), (shard,))
    new_first = first_beta * first_moment + (1.0 - first_beta) * param_grad
    new_second = second_beta * second_moment + (1.0 - second_beta) * param_grad * param_grad
    first_hat = new_first / (1.0 - first_beta**STEP)
    second_hat = new_second / (1.0 - second_beta**STEP)
    new_parameters = parameters - learn_rate * (
        first_hat / (jnp.sqrt(second_hat) + epsilon) + weight_decay * parameters
    )
    return (outputs[None], input_grad[None], param_grad, new_parameters, new_first, new_second)


def solution(mesh):
    in_specs = (
        P("fsdp", "ctx", None),
        P("fsdp", "ctx"),
        P("fsdp", "ctx", None),
        P(("ctx", "fsdp")),
        P(("ctx", "fsdp")),
        P(("ctx", "fsdp")),
    )
    out_specs = (
        P("fsdp", "ctx", None),
        P("fsdp", "ctx", None),
        P(("ctx", "fsdp")),
        P(("ctx", "fsdp")),
        P(("ctx", "fsdp")),
        P(("ctx", "fsdp")),
    )
    return jax.shard_map(
        functools.partial(per_device, mesh.shape["ctx"], mesh.shape["fsdp"]),
        mesh=mesh,
        in_specs=in_specs,
        out_specs=out_specs,
        check_vma=False,
    )
```
